32 devices in a mesh: groups: 1, expert: 8 (over z, core), dp: 4 (over y, x).
Axes of the slice: x: 2, y: 2, z: 4, core: 2. Of those that a mesh axis runs over, the one named last changes fastest.
Arguments:
- tokens: bfloat16 [128, 4096], P(('groups', 'expert', 'dp')), may hold values from -6 to 6
- expert_ids: int32 [128, 2], P(('groups', 'expert', 'dp')), may hold values from 0 to 7, as said below
- gate_weights: bfloat16 [128, 2], P(('groups', 'expert', 'dp')), may hold values from 0.099609375 to 1
- placement: int32 [2, 2], P('groups'), may hold values from 0 to 7, as said below
- w_gate: bfloat16 [8, 1536, 4096], P('expert', 'dp'), may hold values from -0.09375 to 0.09375
- w_up: bfloat16 [8, 1536, 4096], P('expert', 'dp'), may hold values from -0.09375 to 0.09375
- w_down: bfloat16 [8, 1536, 4096], P('expert', 'dp'), may hold values from -0.15625 to 0.15625
Outputs:
- mixed: bfloat16 [128, 4096], P(('groups', 'expert', 'dp'))
The draws below stay inside these ranges and needn't reach their ends.
Inputs may be any that keep to these rules, and one draw needn't show every extreme that they name: `expert_ids`: each row names 2 different experts. In each aligned block of 16 rows (the tokens of one index of expert) no expert is named by more than 6 rows, and some expert is named by exactly that many. `placement`: row 0 holds 2 different experts; row 1 holds 2 different expert indices, none of which appears in row 0.
All inputs are finite; a program needn't handle non-finite values.
Results may differ from the reference program's by a relative error of at most 0.015.
Values may be sent and summed in bfloat16 or wider, within the bound.
A program may use at most 64 MiB of HBM per device.

```python
import math
import jax
import jax.numpy as jnp
from jax import lax

D = 4096
FF = 1536
HOT = 2
EXPERTS = 8
TOPK = 2
GROUP = 16
TOKENS = 128
CAP = 4
OVF = 2
N_EXPERT = 8
N_DP = 4


def listed_pairs(key):
    others = jax.random.permutation(jax.random.fold_in(key, 11), EXPERTS - 1).astype(jnp.int32)
    picked = others[:2 * HOT]
    position = jax.random.randint(jax.random.fold_in(key, 13), (), 0, 2 * HOT).astype(jnp.int32)
    slot_iota = jnp.arange(2 * HOT, dtype=jnp.int32)
    picked = jnp.where(slot_iota == position, EXPERTS - 1, picked).astype(jnp.int32)
    return (picked[:HOT], picked[HOT:2 * HOT])


def draw_placement(key, part):
    chosen, owners = listed_pairs(key)
    return jnp.stack([chosen, owners]).astype(jnp.int32)


def route_block(key, chosen, block_index):
    slots = CAP + OVF
    total = GROUP * TOPK
    block_key = jax.random.fold_in(jax.random.fold_in(key, 23), block_index)
    shuffled = jax.random.permutation(jax.random.fold_in(block_key, 1), EXPERTS).astype(jnp.int32)
    experts_iota = jnp.arange(EXPERTS, dtype=jnp.int32)
    is_listed = jnp.any(experts_iota[:, None] == chosen[None, :], axis=1)
    score = jnp.where(is_listed, 0, 1 + shuffled).astype(jnp.int32)
    order = jnp.argsort(score, stable=True).astype(jnp.int32)
    counts = jnp.clip(total - experts_iota * slots, 0, slots).astype(jnp.int32)
    ends = jnp.cumsum(counts).astype(jnp.int32)
    pair_iota = jnp.arange(total, dtype=jnp.int32)
    which = jnp.sum((pair_iota[:, None] >= ends[None, :]).astype(jnp.int32), axis=1)
    named = order[which]
    grid = named.reshape(TOPK, GROUP).T
    row_order = jax.random.permutation(jax.random.fold_in(block_key, 2), GROUP)
    return grid[row_order].astype(jnp.int32)


def draw_expert_ids(key, part):
    chosen, owners = listed_pairs(key)
    blocks = jax.vmap(lambda index: route_block(key, chosen, index))(jnp.arange(N_EXPERT, dtype=jnp.int32))
    return blocks.reshape(TOKENS, TOPK).astype(jnp.int32)


def level_of(own_key, shape, cuts, low, high):
    gain = 1.0
    for dim, blocks in cuts:
        draws = jax.random.uniform(jax.random.fold_in(jax.random.fold_in(own_key, 6), dim), (blocks,), jnp.float32, low / len(cuts), high / len(cuts))
        gain = gain * jnp.repeat(jnp.exp(draws), shape[dim] // blocks).reshape((-1,) + (1,) * (len(shape) - 1 - dim))
    return gain


def scatter_about(key, dims, width, reach, cuts=(), kind=jnp.bfloat16):
    array = jax.random.normal(key, dims, jnp.float32) * width
    if len(cuts) > 0:
        array = level_of(key, dims, cuts, -0.22, 0.18) * array
    return jnp.clip(array, min=-reach, max=reach).astype(kind)


def setup_inputs(seed: int = 0, part: int = 0) -> dict:
    key_list = jax.random.split(jax.random.key(seed), 8)
    part_keys = jax.random.split(jax.random.fold_in(key_list[7], part), 8)
    return {
        "tokens": scatter_about(part_keys[0], (TOKENS, D), 1.0, 6.0, ((0, 32),)),
        "expert_ids": draw_expert_ids(jax.random.fold_in(jax.random.fold_in(key_list[7], part), 71), part),
        "gate_weights": jnp.clip(jnp.exp(math.log(1.0) - 2.306499 * jax.random.uniform(part_keys[2], (TOKENS, TOPK), jnp.float32) ** level_of(part_keys[2], (TOKENS, TOPK), ((0, 32),), -0.2, 0.2)), 0.099609375, 1.0).astype(jnp.bfloat16),
        "placement": draw_placement(jax.random.fold_in(jax.random.fold_in(key_list[7], part), 71), part),
        "w_gate": scatter_about(key_list[4], (EXPERTS, FF, D), D ** -0.5, 0.09375, ((0, 8), (1, 4))),
        "w_up": scatter_about(key_list[5], (EXPERTS, FF, D), D ** -0.5, 0.09375, ((0, 8), (1, 4))),
        "w_down": scatter_about(key_list[6], (EXPERTS, FF, D), FF ** -0.5, 0.15625, ((0, 8), (1, 4))),
    }


def reference(tokens, expert_ids, gate_weights, placement, w_gate, w_up, w_down):
    slots = CAP + OVF
    pairs = GROUP * TOPK
    flat_ids = expert_ids.reshape(N_EXPERT, pairs)
    onehot = (flat_ids[:, :, None] == jnp.arange(EXPERTS, dtype=jnp.int32)[None, None, :]).astype(jnp.int32)
    before = jnp.cumsum(onehot, axis=1) - onehot
    rank = jnp.sum(before * onehot, axis=2)
    listed = jnp.any(flat_ids[:, :, None] == placement[0][None, None, :], axis=2)
    keep = (rank < CAP) | (listed & (rank < slots))
    group_index = jnp.arange(N_EXPERT, dtype=jnp.int32)[:, None]
    total_rows = EXPERTS * N_EXPERT * slots
    row = flat_ids * (N_EXPERT * slots) + group_index * slots + rank
    row = jnp.where(keep, row, total_rows).astype(jnp.int32).reshape(-1)
    token_index = (group_index * GROUP + jnp.arange(pairs, dtype=jnp.int32)[None, :] // TOPK).astype(jnp.int32).reshape(-1)
    table = jnp.zeros((total_rows + 1,), jnp.int32).at[row].set(token_index)[:-1]
    weight_table = jnp.zeros((total_rows + 1,), jnp.float32).at[row].set(gate_weights.astype(jnp.float32).reshape(-1))[:-1]
    table = table.reshape(EXPERTS, N_EXPERT * slots)
    block = FF // N_DP
    contract = (((1,), (1,)), ((), ()))

    def expert(args):
        index, gate_w, up_w, down_w = args
        rows = tokens[index]
        gate = lax.dot_general(rows, gate_w, contract, preferred_element_type=jnp.float32)
        up = lax.dot_general(rows, up_w, contract, preferred_element_type=jnp.float32)
        hidden = (jax.nn.silu(gate) * up).astype(jnp.bfloat16)
        pieces = jnp.einsum("rbf,bfd->rbd", hidden.reshape(-1, N_DP, block).astype(jnp.float32),
                            down_w.reshape(N_DP, block, D).astype(jnp.float32))
        pieces = pieces.astype(jnp.bfloat16).astype(jnp.float32)
        return jnp.sum(pieces, axis=1)

    results = lax.map(expert, (table, w_gate, w_up, w_down))
    weighted = results.reshape(total_rows, D) * weight_table[:, None]
    mixed = jnp.zeros((TOKENS, D), jnp.float32).at[table.reshape(-1)].add(weighted)
    return mixed.astype(jnp.bfloat16)
```

```python
import functools

import jax
import jax.numpy as jnp
from jax import lax
from jax.experimental import pallas as pl
from jax.experimental.pallas import tpu as pltpu
from jax.sharding import PartitionSpec as P

MESH = pl.DeviceIdType.MESH
F32 = jnp.float32
BF16 = jnp.bfloat16


def each(count, step):
    if count <= 8:
        for i in range(count):
            step(i)
    else:
        def turn(i, carry):
            step(i)
            return carry

        lax.fori_loop(0, count, turn, 0)


def each_from(first, count, step):
    each(count - first, lambda i: step(i + first))


def kernel(experts, dp, topk, first, slots, padded,
           tok, ids, gates, placement, wg_hbm, wu_hbm, wd_hbm, out,
           wg, wu, wd, tok_s, tok_r, info_s, info_r, group_x, disp_s, rows_r, rows_f, part_f,
           part_s, part_r, back_s, back_r, wsel, mix_s, mix_r,
           w_sem, s1, r1, si, ri, s2, r2, s3, r3, s4, r4, s5, r5, s6, r6):
    me_e = lax.axis_index("expert")
    me_j = lax.axis_index("dp")
    own, width = tok.shape
    block = width // dp
    group = own * dp
    pairs = group * topk
    lanes = info_s.shape[1]
    total = experts * padded

    loads = [pltpu.make_async_copy(a, b, w_sem.at[i])
             for i, (a, b) in enumerate(((wg_hbm, wg), (wu_hbm, wu), (wd_hbm, wd)))]
    for load in loads:
        load.start()

    def to_dp(src, dst, send, recv, shift):
        return pltpu.make_async_remote_copy(
            src_ref=src, dst_ref=dst, send_sem=send, recv_sem=recv,
            device_id={"dp": lax.rem(me_j + shift, dp)}, device_id_type=MESH)

    def to_expert(src, dst, send, recv, shift):
        return pltpu.make_async_remote_copy(
            src_ref=src, dst_ref=dst, send_sem=send, recv_sem=recv,
            device_id={"expert": lax.rem(me_e + shift, experts)}, device_id_type=MESH)

    def cols(j):
        return pl.ds(pl.multiple_of(j * block, 128), block)

    barrier = pltpu.get_barrier_semaphore()
    for s in range(1, dp):
        pl.semaphore_signal(barrier, inc=1, device_id={"dp": lax.rem(me_j + s, dp)}, device_id_type=MESH)

    def greet(d):
        pl.semaphore_signal(barrier, inc=1, device_id={"expert": lax.rem(me_e + d, experts)}, device_id_type=MESH)

    each_from(1, experts, greet)

    lane = lax.broadcasted_iota(jnp.int32, (8, lanes), 1)
    line = lax.broadcasted_iota(jnp.int32, (8, lanes), 0)
    id_f = ids[...].astype(F32)
    gate_f = gates[...].astype(F32)
    info = jnp.zeros((8, lanes), F32)
    for t in range(own):
        for k in range(topk):
            here = lane == (me_j * own + t) * topk + k
            value = jnp.where(line == 0, jnp.broadcast_to(id_f[t:t + 1, k:k + 1], (8, lanes)),
                              jnp.broadcast_to(gate_f[t:t + 1, k:k + 1], (8, lanes)))
            info = jnp.where(here, value, info)
    info_s[...] = info
    for s in range(1, dp):
        tok_s[s] = tok[:, cols(lax.rem(me_j + s, dp))]
    tok_r[me_j] = tok[:, cols(me_j)]

    pl.semaphore_wait(barrier, dp - 1 + experts - 1)

    for s in range(1, dp):
        to_dp(info_s, info_r.at[s], si.at[s], ri.at[s], s).start()
    for s in range(1, dp):
        to_dp(tok_s.at[s], tok_r.at[me_j], s1.at[s], r1.at[s], s).start()
    for s in range(1, dp):
        to_dp(info_s, info_r.at[s], si.at[s], ri.at[s], s).wait_recv()
        info = info + info_r[s]

    id_row = info[0:1, :]
    gate_row = info[1:2, :]
    at_row = lax.broadcasted_iota(jnp.int32, (pairs, lanes), 0)
    at_lane = lax.broadcasted_iota(jnp.int32, (pairs, lanes), 1)
    id_col = jnp.sum(jnp.where(at_row == at_lane, jnp.broadcast_to(id_row, (pairs, lanes)), 0.0),
                     axis=1, keepdims=True)
    same = jnp.broadcast_to(id_col, (pairs, lanes)) == jnp.broadcast_to(id_row, (pairs, lanes))
    rank = jnp.sum(jnp.where(same, jnp.where(at_row < at_lane, 1.0, 0.0), 0.0), axis=0, keepdims=True)
    limit = jnp.full((1, lanes), float(first), F32)
    for h in range(placement.shape[1]):
        limit = jnp.where(id_row == placement[0, h].astype(F32), float(slots), limit)
    dest = jnp.where(rank < limit, id_row * float(padded) + rank, -1.0)
    dest = jnp.where(lax.broadcasted_iota(jnp.int32, (1, lanes), 1) < pairs, dest, -1.0)
    pick = lax.broadcasted_iota(jnp.int32, (total, lanes), 0).astype(F32) == jnp.broadcast_to(dest, (total, lanes))
    pair_i = lax.broadcasted_iota(jnp.int32, (lanes, group), 0)
    token_i = lax.broadcasted_iota(jnp.int32, (lanes, group), 1) * topk
    fold = jnp.where(pair_i >= token_i, jnp.where(pair_i < token_i + topk, 1.0, 0.0), 0.0).astype(BF16)
    select = jnp.dot(jnp.where(pick, 1.0, 0.0).astype(BF16), fold, preferred_element_type=F32).astype(BF16)
    wsel[...] = jnp.dot(jnp.where(pick, jnp.broadcast_to(gate_row, (total, lanes)), 0.0).astype(BF16), fold,
                        preferred_element_type=F32)

    for s in range(1, dp):
        to_dp(tok_s.at[s], tok_r.at[lax.rem(me_j + dp - s, dp)], s1.at[s], r1.at[s], s).wait_recv()
    for j in range(dp):
        group_x[j * own:(j + 1) * own, :] = tok_r[j].astype(F32)
    rows_f[...] = jnp.dot(select, group_x[...].astype(BF16), preferred_element_type=F32)

    def dispatch(d):
        e = lax.rem(me_e + d, experts)
        start = pl.multiple_of(e * padded, 8)
        disp_s[e] = rows_f[pl.ds(start, slots), :].astype(BF16)
        to_expert(disp_s.at[e], rows_r.at[me_j, me_e], s2.at[d], r2.at[d], d).start()

    each_from(1, experts, dispatch)
    rows_r[me_j, me_e] = rows_f[pl.ds(pl.multiple_of(me_e * padded, 8), slots), :].astype(BF16)

    def forward(d):
        g = lax.rem(me_e + experts - d, experts)
        for s in range(1, dp):
            to_dp(rows_r.at[me_j, g], rows_r.at[me_j, g], s3.at[s, d], r3.at[s, d], s).start()

    forward(0)

    def arrive(d):
        g = lax.rem(me_e + experts - d, experts)
        to_expert(disp_s.at[g], rows_r.at[me_j, g], s2.at[d], r2.at[d], d).wait_recv()
        forward(d)

    each_from(1, experts, arrive)

    loads[0].wait()
    loads[1].wait()
    contract = (((1,), (1,)), ((), ()))
    gate = up = None
    for s in range(dp):
        j = lax.rem(me_j + dp - s, dp)

        def take(d):
            g = lax.rem(me_e + experts - d, experts)
            if s > 0:
                to_dp(rows_r.at[j, g], rows_r.at[j, g], s3.at[s, d], r3.at[s, d], s).wait_recv()
            rows_f[pl.ds(pl.multiple_of(g * padded, 8), slots), :] = rows_r[j, g].astype(F32)

        each(experts, take)
        x = rows_f[...].astype(BF16)
        gate_part = lax.dot_general(x, wg[:, cols(j)], contract, preferred_element_type=F32)
        up_part = lax.dot_general(x, wu[:, cols(j)], contract, preferred_element_type=F32)
        gate = gate_part if gate is None else gate + gate_part
        up = up_part if up is None else up + up_part
    hidden = (gate / (1.0 + jnp.exp(-gate)) * up).astype(BF16)

    loads[2].wait()
    for s in list(range(1, dp)) + [0]:
        j = lax.rem(me_j + s, dp)
        part_f[...] = jnp.dot(hidden, wd[:, cols(j)], preferred_element_type=F32)
        target = part_s if s > 0 else part_r

        def split(g):
            target[s, g] = part_f[pl.ds(g * padded, slots), :].astype(BF16)

        each(experts, split)
        if s > 0:
            to_dp(part_s.at[s], part_r.at[s], s4.at[s], r4.at[s], s).start()
    for s in range(1, dp):
        to_dp(part_s.at[s], part_r.at[s], s4.at[s], r4.at[s], s).wait_recv()

    def summed(g):
        value = part_r[0, g].astype(F32)
        for s in range(1, dp):
            value = value + part_r[s, g].astype(F32)
        return value.astype(BF16)

    def give(d):
        g = lax.rem(me_e + d, experts)
        back_s[g] = summed(g)
        to_expert(back_s.at[g], back_r.at[me_e], s5.at[d], r5.at[d], d).start()

    each_from(1, experts, give)
    back_r[me_e] = summed(me_e)

    def collect(d):
        e = lax.rem(me_e + experts - d, experts)
        to_expert(back_s.at[e], back_r.at[e], s5.at[d], r5.at[d], d).wait_recv()

    each_from(1, experts, collect)

    def place(e):
        rows_f[pl.ds(e * padded, slots), :] = back_r[e].astype(F32)

    each(experts, place)
    group_x[...] = lax.dot_general(wsel[...].astype(BF16), rows_f[...].astype(BF16), (((0,), (0,)), ((), ())),
                                   preferred_element_type=F32)
    for j in range(dp):
        mix_s[j] = group_x[j * own:(j + 1) * own, :].astype(BF16)
    for s in range(1, dp):
        to_dp(mix_s.at[lax.rem(me_j + s, dp)], mix_r.at[me_j], s6.at[s], r6.at[s], s).start()
    mix_r[me_j] = mix_s[me_j]
    for s in range(1, dp):
        j = lax.rem(me_j + dp - s, dp)
        to_dp(mix_s.at[j], mix_r.at[j], s6.at[s], r6.at[s], s).wait_recv()
    for j in range(dp):
        out[:, j * block:(j + 1) * block] = mix_r[j]

    for s in range(1, dp):
        to_dp(info_s, info_r.at[s], si.at[s], ri.at[s], s).wait_send()
        to_dp(tok_s.at[s], tok_r.at[me_j], s1.at[s], r1.at[s], s).wait_send()
        to_dp(part_s.at[s], part_r.at[s], s4.at[s], r4.at[s], s).wait_send()
        to_dp(mix_s.at[lax.rem(me_j + s, dp)], mix_r.at[me_j], s6.at[s], r6.at[s], s).wait_send()

    def left(d):
        g = lax.rem(me_e + experts - d, experts)
        for s in range(1, dp):
            to_dp(rows_r.at[me_j, g], rows_r.at[me_j, g], s3.at[s, d], r3.at[s, d], s).wait_send()

    def left_expert(d):
        e = lax.rem(me_e + d, experts)
        to_expert(disp_s.at[e], rows_r.at[me_j, me_e], s2.at[d], r2.at[d], d).wait_send()
        to_expert(back_s.at[e], back_r.at[me_e], s5.at[d], r5.at[d], d).wait_send()

    each(experts, left)
    each_from(1, experts, left_expert)


def body(tokens, expert_ids, gate_weights, placement, w_gate, w_up, w_down):
    experts = lax.axis_size("expert")
    dp = lax.axis_size("dp")
    own, width = tokens.shape
    topk = expert_ids.shape[1]
    group = own * dp
    first = max(2, group * topk // experts)
    slots = first + max(1, first // 2)
    padded = -(-slots // 8) * 8
    lanes = -(-group * topk // 128) * 128
    block = width // dp
    units = w_gate.shape[1]
    total = experts * padded
    vmem = pl.BlockSpec(memory_space=pltpu.VMEM)
    smem = pl.BlockSpec(memory_space=pltpu.SMEM)
    hbm = pl.BlockSpec(memory_space=pl.ANY)
    dma = pltpu.SemaphoreType.DMA
    return pl.pallas_call(
        functools.partial(kernel, experts, dp, topk, first, slots, padded),
        out_shape=jax.ShapeDtypeStruct((own, width), BF16),
        in_specs=[vmem, vmem, vmem, smem, hbm, hbm, hbm],
        out_specs=vmem,
        scratch_shapes=[
            pltpu.VMEM((units, width), BF16),
            pltpu.VMEM((units, width), BF16),
            pltpu.VMEM((units, width), BF16),
            pltpu.VMEM((dp, own, block), BF16),
            pltpu.VMEM((dp, own, block), BF16),
            pltpu.VMEM((8, lanes), F32),
            pltpu.VMEM((dp, 8, lanes), F32),
            pltpu.VMEM((group, block), F32),
            pltpu.VMEM((experts, slots, block), BF16),
            pltpu.VMEM((dp, experts, slots, block), BF16),
            pltpu.VMEM((total, block), F32),
            pltpu.VMEM((total, block), F32),
            pltpu.VMEM((dp, experts, slots, block), BF16),
            pltpu.VMEM((dp, experts, slots, block), BF16),
            pltpu.VMEM((experts, slots, block), BF16),
            pltpu.VMEM((experts, slots, block), BF16),
            pltpu.VMEM((total, group), F32),
            pltpu.VMEM((dp, own, block), BF16),
            pltpu.VMEM((dp, own, block), BF16),
            dma((3,)),
            dma((dp,)), dma((dp,)), dma((dp,)), dma((dp,)),
            dma((experts,)), dma((experts,)),
            dma((dp, experts)), dma((dp, experts)),
            dma((dp,)), dma((dp,)),
            dma((experts,)), dma((experts,)),
            dma((dp,)), dma((dp,)),
        ],
        compiler_params=pltpu.CompilerParams(
            collective_id=0, has_side_effects=True, vmem_limit_bytes=56 * 1024 * 1024
        ),
    )(tokens, expert_ids, gate_weights, placement, w_gate[0], w_up[0], w_down[0])


def solution(mesh):
    placed = (
        P(("groups", "expert", "dp"), None),
        P(("groups", "expert", "dp"), None),
        P(("groups", "expert", "dp"), None),
        P("groups", None),
        P("expert", "dp", None),
        P("expert", "dp", None),
        P("expert", "dp", None),
    )
    return jax.shard_map(
        body,
        mesh=mesh,
        in_specs=placed,
        out_specs=P(("groups", "expert", "dp"), None),
        check_vma=False,
    )
```

```python
import functools

import jax
import jax.numpy as jnp
from jax import lax
from jax.experimental import pallas as pl
from jax.experimental.pallas import tpu as pltpu
from jax.sharding import PartitionSpec as P

MESH = pl.DeviceIdType.MESH
F32 = jnp.float32
BF16 = jnp.bfloat16


def each(count, step):
    if count <= 8:
        for i in range(count):
            step(i)
    else:
        def turn(i, carry):
            step(i)
            return carry

        lax.fori_loop(0, count, turn, 0)


def each_from(first, count, step):
    each(count - first, lambda i: step(i + first))


def kernel(experts, dp, topk, first, slots, padded,
           tok_hbm, ids_hbm, gates_hbm, placement_hbm, wg_hbm, wu_hbm, wd_hbm, out,
           tok, ids, gates, placement,
           wg, wu, wd, tok_s, tok_r, info_s, info_r, group_x, disp_s, rows_r, rows_f, part_f,
           part_s, part_r, back_s, back_r, wsel, mix_s, mix_r,
           w_sem, s1, r1, si, ri, s2, r2, s3, r3, s4, r4, s5, r5, s6, r6):
    me_e = lax.axis_index("expert")
    me_j = lax.axis_index("dp")
    own, width = tok.shape
    block = width // dp
    group = own * dp
    pairs = group * topk
    lanes = info_s.shape[1]
    total = experts * padded

    def to_dp(src, dst, send, recv, shift):
        return pltpu.make_async_remote_copy(
            src_ref=src, dst_ref=dst, send_sem=send, recv_sem=recv,
            device_id={"dp": lax.rem(me_j + shift, dp)}, device_id_type=MESH)

    def to_expert(src, dst, send, recv, shift):
        return pltpu.make_async_remote_copy(
            src_ref=src, dst_ref=dst, send_sem=send, recv_sem=recv,
            device_id={"expert": lax.rem(me_e + shift, experts)}, device_id_type=MESH)

    def cols(j):
        return pl.ds(pl.multiple_of(j * block, 128), block)

    barrier = pltpu.get_barrier_semaphore()
    for s in range(1, dp):
        pl.semaphore_signal(barrier, inc=1, device_id={"dp": lax.rem(me_j + s, dp)}, device_id_type=MESH)

    def greet(d):
        pl.semaphore_signal(barrier, inc=1, device_id={"expert": lax.rem(me_e + d, experts)}, device_id_type=MESH)

    each_from(1, experts, greet)

    pairs_of = ((ids_hbm, ids), (gates_hbm, gates), (placement_hbm, placement), (tok_hbm, tok),
                (wg_hbm, wg), (wu_hbm, wu), (wd_hbm, wd))
    loads = [pltpu.make_async_copy(a, b, w_sem.at[i]) for i, (a, b) in enumerate(pairs_of)]
    for load in loads:
        load.start()
    for load in loads[:4]:
        load.wait()
    loads = loads[4:]

    lane = lax.broadcasted_iota(jnp.int32, (8, lanes), 1)
    line = lax.broadcasted_iota(jnp.int32, (8, lanes), 0)
    id_f = ids[...].astype(F32)
    gate_f = gates[...].astype(F32)
    info = jnp.zeros((8, lanes), F32)
    for t in range(own):
        for k in range(topk):
            here = lane == (me_j * own + t) * topk + k
            value = jnp.where(line == 0, jnp.broadcast_to(id_f[k:k + 1, t:t + 1], (8, lanes)),
                              jnp.broadcast_to(gate_f[k:k + 1, t:t + 1], (8, lanes)))
            info = jnp.where(here, value, info)
    info_s[...] = info
    for s in range(1, dp):
        tok_s[s] = tok[:, cols(lax.rem(me_j + s, dp))]
    tok_r[me_j] = tok[:, cols(me_j)]

    pl.semaphore_wait(barrier, dp - 1 + experts - 1)

    for s in range(1, dp):
        to_dp(info_s, info_r.at[s], si.at[s], ri.at[s], s).start()
    for s in range(1, dp):
        to_dp(tok_s.at[s], tok_r.at[me_j], s1.at[s], r1.at[s], s).start()
    for s in range(1, dp):
        to_dp(info_s, info_r.at[s], si.at[s], ri.at[s], s).wait_recv()
        info = info + info_r[s]

    id_row = info[0:1, :]
    gate_row = info[1:2, :]
    at_row = lax.broadcasted_iota(jnp.int32, (pairs, lanes), 0)
    at_lane = lax.broadcasted_iota(jnp.int32, (pairs, lanes), 1)
    id_col = jnp.sum(jnp.where(at_row == at_lane, jnp.broadcast_to(id_row, (pairs, lanes)), 0.0),
                     axis=1, keepdims=True)
    same = jnp.broadcast_to(id_col, (pairs, lanes)) == jnp.broadcast_to(id_row, (pairs, lanes))
    rank = jnp.sum(jnp.where(same, jnp.where(at_row < at_lane, 1.0, 0.0), 0.0), axis=0, keepdims=True)
    limit = jnp.full((1, lanes), float(first), F32)
    listed = placement[...].astype(F32)
    for h in range(placement.shape[1]):
        limit = jnp.where(id_row == jnp.broadcast_to(listed[0:1, h:h + 1], (1, lanes)), float(slots), limit)
    dest = jnp.where(rank < limit, id_row * float(padded) + rank, -1.0)
    dest = jnp.where(lax.broadcasted_iota(jnp.int32, (1, lanes), 1) < pairs, dest, -1.0)
    pick = lax.broadcasted_iota(jnp.int32, (total, lanes), 0).astype(F32) == jnp.broadcast_to(dest, (total, lanes))
    pair_i = lax.broadcasted_iota(jnp.int32, (lanes, group), 0)
    token_i = lax.broadcasted_iota(jnp.int32, (lanes, group), 1) * topk
    fold = jnp.where(pair_i >= token_i, jnp.where(pair_i < token_i + topk, 1.0, 0.0), 0.0).astype(BF16)
    select = jnp.dot(jnp.where(pick, 1.0, 0.0).astype(BF16), fold, preferred_element_type=F32).astype(BF16)

    for s in range(1, dp):
        to_dp(tok_s.at[s], tok_r.at[lax.rem(me_j + dp - s, dp)], s1.at[s], r1.at[s], s).wait_recv()
    for j in range(dp):
        group_x[j * own:(j + 1) * own, :] = tok_r[j].astype(F32)
    rows_f[...] = jnp.dot(select, group_x[...].astype(BF16), preferred_element_type=F32)

    def dispatch(d):
        e = lax.rem(me_e + d, experts)
        start = pl.multiple_of(e * padded, 8)
        disp_s[e] = rows_f[pl.ds(start, slots), :].astype(BF16)
        to_expert(disp_s.at[e], rows_r.at[me_j, me_e], s2.at[d], r2.at[d], d).start()

    each_from(1, experts, dispatch)
    rows_r[me_j, me_e] = rows_f[pl.ds(pl.multiple_of(me_e * padded, 8), slots), :].astype(BF16)

    def forward(d):
        g = lax.rem(me_e + experts - d, experts)
        for s in range(1, dp):
            to_dp(rows_r.at[me_j, g], rows_r.at[me_j, g], s3.at[s, d], r3.at[s, d], s).start()

    forward(0)
    wsel[...] = jnp.dot(jnp.where(pick, jnp.broadcast_to(gate_row, (total, lanes)), 0.0).astype(BF16), fold,
                        preferred_element_type=F32)


    def arrive(d):
        g = lax.rem(me_e + experts - d, experts)
        to_expert(disp_s.at[g], rows_r.at[me_j, g], s2.at[d], r2.at[d], d).wait_recv()
        forward(d)

    each_from(1, experts, arrive)

    loads[0].wait()
    loads[1].wait()
    contract = (((1,), (1,)), ((), ()))
    gate = up = None
    for s in range(dp):
        j = lax.rem(me_j + dp - s, dp)

        def take(d):
            g = lax.rem(me_e + experts - d, experts)
            if s > 0:
                to_dp(rows_r.at[j, g], rows_r.at[j, g], s3.at[s, d], r3.at[s, d], s).wait_recv()
            rows_f[pl.ds(pl.multiple_of(g * padded, 8), slots), :] = rows_r[j, g].astype(F32)

        each(experts, take)
        x = rows_f[...].astype(BF16)
        gate_part = lax.dot_general(x, wg[:, cols(j)], contract, preferred_element_type=F32)
        up_part = lax.dot_general(x, wu[:, cols(j)], contract, preferred_element_type=F32)
        gate = gate_part if gate is None else gate + gate_part
        up = up_part if up is None else up + up_part
    hidden = (gate / (1.0 + jnp.exp(-gate)) * up).astype(BF16)

    loads[2].wait()
    for s in list(range(1, dp)) + [0]:
        j = lax.rem(me_j + s, dp)
        part_f[...] = jnp.dot(hidden, wd[:, cols(j)], preferred_element_type=F32)
        target = part_s if s > 0 else part_r

        def split(d):
            g = lax.rem(me_e + d, experts)
            start = pl.multiple_of(g * padded, 8)
            target[s, g] = part_f[pl.ds(start, slots), :].astype(BF16)
            if s > 0:
                to_dp(part_s.at[s, g], part_r.at[s, g], s4.at[s, d], r4.at[s, d], s).start()

        each_from(1, experts, split)
        split(0)

    def summed(d):
        g = lax.rem(me_e + d, experts)
        for s in range(1, dp):
            to_dp(part_s.at[s, g], part_r.at[s, g], s4.at[s, d], r4.at[s, d], s).wait_recv()
        value = part_r[0, g].astype(F32)
        for s in range(1, dp):
            value = value + part_r[s, g].astype(F32)
        return value.astype(BF16)

    def give(d):
        g = lax.rem(me_e + d, experts)
        back_s[g] = summed(d)
        to_expert(back_s.at[g], back_r.at[me_e], s5.at[d], r5.at[d], d).start()

    each_from(1, experts, give)
    back_r[me_e] = summed(0)

    def collect(d):
        e = lax.rem(me_e + experts - d, experts)
        to_expert(back_s.at[e], back_r.at[e], s5.at[d], r5.at[d], d).wait_recv()

    each_from(1, experts, collect)

    def place(e):
        rows_f[pl.ds(e * padded, slots), :] = back_r[e].astype(F32)

    each(experts, place)
    group_x[...] = lax.dot_general(wsel[...].astype(BF16), rows_f[...].astype(BF16), (((0,), (0,)), ((), ())),
                                   preferred_element_type=F32)
    for j in range(dp):
        mix_s[j] = group_x[j * own:(j + 1) * own, :].astype(BF16)
    for s in range(1, dp):
        to_dp(mix_s.at[lax.rem(me_j + s, dp)], mix_r.at[me_j], s6.at[s], r6.at[s], s).start()
    mix_r[me_j] = mix_s[me_j]
    for s in range(1, dp):
        j = lax.rem(me_j + dp - s, dp)
        to_dp(mix_s.at[j], mix_r.at[j], s6.at[s], r6.at[s], s).wait_recv()
    for j in range(dp):
        out[:, j * block:(j + 1) * block] = mix_r[j]

    for s in range(1, dp):
        to_dp(info_s, info_r.at[s], si.at[s], ri.at[s], s).wait_send()
        to_dp(tok_s.at[s], tok_r.at[me_j], s1.at[s], r1.at[s], s).wait_send()
        to_dp(mix_s.at[lax.rem(me_j + s, dp)], mix_r.at[me_j], s6.at[s], r6.at[s], s).wait_send()

    def left(d):
        g = lax.rem(me_e + experts - d, experts)
        for s in range(1, dp):
            to_dp(rows_r.at[me_j, g], rows_r.at[me_j, g], s3.at[s, d], r3.at[s, d], s).wait_send()
            to_dp(part_s.at[s, g], part_r.at[s, g], s4.at[s, d], r4.at[s, d], s).wait_send()

    def left_expert(d):
        e = lax.rem(me_e + d, experts)
        to_expert(disp_s.at[e], rows_r.at[me_j, me_e], s2.at[d], r2.at[d], d).wait_send()
        to_expert(back_s.at[e], back_r.at[me_e], s5.at[d], r5.at[d], d).wait_send()

    each(experts, left)
    each_from(1, experts, left_expert)


def body(tokens, expert_ids, gate_weights, placement, w_gate, w_up, w_down):
    experts = lax.axis_size("expert")
    dp = lax.axis_size("dp")
    own, width = tokens.shape
    topk = expert_ids.shape[1]
    group = own * dp
    first = max(2, group * topk // experts)
    slots = first + max(1, first // 2)
    padded = -(-slots // 8) * 8
    lanes = -(-group * topk // 128) * 128
    block = width // dp
    units = w_gate.shape[1]
    total = experts * padded
    vmem = pl.BlockSpec(memory_space=pltpu.VMEM)
    hbm = pl.BlockSpec(memory_space=pl.ANY)
    dma = pltpu.SemaphoreType.DMA
    return pl.pallas_call(
        functools.partial(kernel, experts, dp, topk, first, slots, padded),
        out_shape=jax.ShapeDtypeStruct((own, width), BF16),
        in_specs=[hbm] * 7,
        out_specs=vmem,
        scratch_shapes=[
            pltpu.VMEM((own, width), BF16),
            pltpu.VMEM((topk, own), jnp.int32),
            pltpu.VMEM((topk, own), BF16),
            pltpu.VMEM(placement.shape, jnp.int32),
            pltpu.VMEM((units, width), BF16),
            pltpu.VMEM((units, width), BF16),
            pltpu.VMEM((units, width), BF16),
            pltpu.VMEM((dp, own, block), BF16),
            pltpu.VMEM((dp, own, block), BF16),
            pltpu.VMEM((8, lanes), F32),
            pltpu.VMEM((dp, 8, lanes), F32),
            pltpu.VMEM((group, block), F32),
            pltpu.VMEM((experts, slots, block), BF16),
            pltpu.VMEM((dp, experts, slots, block), BF16),
            pltpu.VMEM((total, block), F32),
            pltpu.VMEM((total, block), F32),
            pltpu.VMEM((dp, experts, slots, block), BF16),
            pltpu.VMEM((dp, experts, slots, block), BF16),
            pltpu.VMEM((experts, slots, block), BF16),
            pltpu.VMEM((experts, slots, block), BF16),
            pltpu.VMEM((total, group), F32),
            pltpu.VMEM((dp, own, block), BF16),
            pltpu.VMEM((dp, own, block), BF16),
            dma((7,)),
            dma((dp,)), dma((dp,)), dma((dp,)), dma((dp,)),
            dma((experts,)), dma((experts,)),
            dma((dp, experts)), dma((dp, experts)),
            dma((dp, experts)), dma((dp, experts)),
            dma((experts,)), dma((experts,)),
            dma((dp,)), dma((dp,)),
        ],
        compiler_params=pltpu.CompilerParams(
            collective_id=0, has_side_effects=True, vmem_limit_bytes=56 << 20
        ),
    )(tokens, expert_ids.T, gate_weights.T, placement, w_gate[0], w_up[0], w_down[0])


def solution(mesh):
    placed = (
        P(("groups", "expert", "dp"), None),
        P(("groups", "expert", "dp"), None),
        P(("groups", "expert", "dp"), None),
        P("groups", None),
        P("expert", "dp", None),
        P("expert", "dp", None),
        P("expert", "dp", None),
    )
    return jax.shard_map(
        body,
        mesh=mesh,
        in_specs=placed,
        out_specs=P(("groups", "expert", "dp"), None),
        check_vma=False,
    )
```

```python
import functools

import jax
import jax.numpy as jnp
from jax import lax
from jax.experimental import pallas as pl
from jax.experimental.pallas import tpu as pltpu
from jax.sharding import PartitionSpec as P

MESH = pl.DeviceIdType.MESH
F32 = jnp.float32
BF16 = jnp.bfloat16


def each(count, step):
    if count <= 8:
        for i in range(count):
            step(i)
    else:
        def turn(i, carry):
            step(i)
            return carry

        lax.fori_loop(0, count, turn, 0)


def each_from(first, count, step):
    each(count - first, lambda i: step(i + first))


def kernel(experts, dp, topk, first, slots, padded,
           tok_hbm, ids_hbm, gates_hbm, placement_hbm, wg_hbm, wu_hbm, wd_hbm, out,
           tok, ids, gates, placement,
           wg, wu, wd, tok_s, tok_r, info_s, info_r, group_x, disp_s, rows_r, rows_f, part_f,
           part_s, part_r, back_s, back_r, wsel, mix_s,
           w_sem, s1, r1, si, ri, s2, r2, s3, r3, s4, r4, s5, r5, s6, r6):
    me_e = lax.axis_index("expert")
    me_j = lax.axis_index("dp")
    own, width = tok.shape
    block = width // dp
    group = own * dp
    pairs = group * topk
    lanes = info_s.shape[1]
    total = experts * padded

    if dp == 4:
        low, high = lax.rem(me_j, 2), me_j // 2
        across = (me_j, high * 2 + (1 - low), (1 - high) * 2 + low, (1 - high) * 2 + (1 - low))
        onward = backward = lambda s: across[s]
    else:
        onward = lambda s: lax.rem(me_j + s, dp)
        backward = lambda s: lax.rem(me_j + dp - s, dp)

    def to_dp(src, dst, send, recv, s):
        return pltpu.make_async_remote_copy(
            src_ref=src, dst_ref=dst, send_sem=send, recv_sem=recv,
            device_id={"dp": onward(s)}, device_id_type=MESH)

    def to_expert(src, dst, send, recv, shift):
        return pltpu.make_async_remote_copy(
            src_ref=src, dst_ref=dst, send_sem=send, recv_sem=recv,
            device_id={"expert": lax.rem(me_e + shift, experts)}, device_id_type=MESH)

    def cols(j):
        return pl.ds(pl.multiple_of(j * block, 128), block)

    barrier = pltpu.get_barrier_semaphore()
    for s in range(1, dp):
        pl.semaphore_signal(barrier, inc=1, device_id={"dp": onward(s)}, device_id_type=MESH)

    def greet(d):
        pl.semaphore_signal(barrier, inc=1, device_id={"expert": lax.rem(me_e + d, experts)}, device_id_type=MESH)

    each_from(1, experts, greet)

    pairs_of = ((ids_hbm, ids), (gates_hbm, gates), (placement_hbm, placement), (tok_hbm, tok),
                (wg_hbm, wg), (wu_hbm, wu), (wd_hbm, wd))
    loads = [pltpu.make_async_copy(a, b, w_sem.at[i]) for i, (a, b) in enumerate(pairs_of)]
    for load in loads:
        load.start()
    for load in loads[:4]:
        load.wait()
    loads = loads[4:]

    lane = lax.broadcasted_iota(jnp.int32, (8, lanes), 1)
    line = lax.broadcasted_iota(jnp.int32, (8, lanes), 0)
    id_f = ids[...].astype(F32)
    gate_f = gates[...].astype(F32)
    info = jnp.zeros((8, lanes), F32)
    for t in range(own):
        for k in range(topk):
            here = lane == (me_j * own + t) * topk + k
            value = jnp.where(line == 0, jnp.broadcast_to(id_f[k:k + 1, t:t + 1], (8, lanes)),
                              jnp.broadcast_to(gate_f[k:k + 1, t:t + 1], (8, lanes)))
            info = jnp.where(here, value, info)
    info_s[...] = info
    for s in range(1, dp):
        tok_s[s] = tok[:, cols(onward(s))]
    tok_r[me_j] = tok[:, cols(me_j)]

    pl.semaphore_wait(barrier, dp - 1 + experts - 1)

    for s in range(1, dp):
        to_dp(info_s, info_r.at[s], si.at[s], ri.at[s], s).start()
    for s in range(1, dp):
        to_dp(tok_s.at[s], tok_r.at[me_j], s1.at[s], r1.at[s], s).start()
    for s in range(1, dp):
        to_dp(info_s, info_r.at[s], si.at[s], ri.at[s], s).wait_recv()
        info = info + info_r[s]

    id_row = info[0:1, :]
    gate_row = info[1:2, :]
    at_row = lax.broadcasted_iota(jnp.int32, (pairs, lanes), 0)
    at_lane = lax.broadcasted_iota(jnp.int32, (pairs, lanes), 1)
    id_col = jnp.sum(jnp.where(at_row == at_lane, jnp.broadcast_to(id_row, (pairs, lanes)), 0.0),
                     axis=1, keepdims=True)
    same = jnp.broadcast_to(id_col, (pairs, lanes)) == jnp.broadcast_to(id_row, (pairs, lanes))
    rank = jnp.sum(jnp.where(same, jnp.where(at_row < at_lane, 1.0, 0.0), 0.0), axis=0, keepdims=True)
    limit = jnp.full((1, lanes), float(first), F32)
    listed = placement[...].astype(F32)
    for h in range(placement.shape[1]):
        limit = jnp.where(id_row == jnp.broadcast_to(listed[0:1, h:h + 1], (1, lanes)), float(slots), limit)
    dest = jnp.where(rank < limit, id_row * float(padded) + rank, -1.0)
    dest = jnp.where(lax.broadcasted_iota(jnp.int32, (1, lanes), 1) < pairs, dest, -1.0)
    pick = lax.broadcasted_iota(jnp.int32, (total, lanes), 0).astype(F32) == jnp.broadcast_to(dest, (total, lanes))
    pair_i = lax.broadcasted_iota(jnp.int32, (lanes, group), 0)
    token_i = lax.broadcasted_iota(jnp.int32, (lanes, group), 1) * topk
    fold = jnp.where(pair_i >= token_i, jnp.where(pair_i < token_i + topk, 1.0, 0.0), 0.0).astype(BF16)
    select = jnp.dot(jnp.where(pick, 1.0, 0.0).astype(BF16), fold, preferred_element_type=F32).astype(BF16)

    for s in range(1, dp):
        to_dp(tok_s.at[s], tok_r.at[backward(s)], s1.at[s], r1.at[s], s).wait_recv()
    for j in range(dp):
        group_x[j * own:(j + 1) * own, :] = tok_r[j].astype(F32)
    rows_f[...] = jnp.dot(select, group_x[...].astype(BF16), preferred_element_type=F32)

    def dispatch(d):
        e = lax.rem(me_e + d, experts)
        start = pl.multiple_of(e * padded, 8)
        disp_s[e] = rows_f[pl.ds(start, slots), :].astype(BF16)
        to_expert(disp_s.at[e], rows_r.at[me_j, me_e], s2.at[d], r2.at[d], d).start()

    each_from(1, experts, dispatch)
    rows_r[me_j, me_e] = rows_f[pl.ds(pl.multiple_of(me_e * padded, 8), slots), :].astype(BF16)

    relayed = dp == 4 and experts <= 8
    direct = (1, 2) if relayed else range(1, dp)

    def forward(d):
        g = lax.rem(me_e + experts - d, experts)
        for s in direct:
            to_dp(rows_r.at[me_j, g], rows_r.at[me_j, g], s3.at[s, d], r3.at[s, d], s).start()

    forward(0)
    wsel[...] = jnp.dot(jnp.where(pick, jnp.broadcast_to(gate_row, (total, lanes)), 0.0).astype(BF16), fold,
                        preferred_element_type=F32)


    def arrive(d):
        g = lax.rem(me_e + experts - d, experts)
        to_expert(disp_s.at[g], rows_r.at[me_j, g], s2.at[d], r2.at[d], d).wait_recv()
        forward(d)

    each_from(1, experts, arrive)

    loads[0].wait()
    loads[1].wait()
    contract = (((1,), (1,)), ((), ()))

    def first_of(d):
        return 1 + d % 2

    def relay(d):
        g = lax.rem(me_e + experts - d, experts)
        side = first_of(d)
        j = onward(side)
        to_dp(rows_r.at[j, g], rows_r.at[j, g], s3.at[side, d], r3.at[side, d], side).wait_recv()
        to_dp(rows_r.at[j, g], rows_r.at[j, g], s3.at[3, d], r3.at[3, d], 3 - side).start()

    gate = up = None
    for s in range(dp):
        j = backward(s)

        def take(d):
            g = lax.rem(me_e + experts - d, experts)
            if s > 0 and not (relayed and s == first_of(d)):
                to_dp(rows_r.at[j, g], rows_r.at[j, g], s3.at[s, d], r3.at[s, d], s).wait_recv()
            rows_f[pl.ds(pl.multiple_of(g * padded, 8), slots), :] = rows_r[j, g].astype(F32)

        each(experts, take)
        x = rows_f[...].astype(BF16)
        gate_part = lax.dot_general(x, wg[:, cols(j)], contract, preferred_element_type=F32)
        up_part = lax.dot_general(x, wu[:, cols(j)], contract, preferred_element_type=F32)
        gate = gate_part if gate is None else gate + gate_part
        up = up_part if up is None else up + up_part
        if relayed and s == 0:
            each(experts, relay)
    hidden = (gate / (1.0 + jnp.exp(-gate)) * up).astype(BF16)

    loads[2].wait()
    for s in reversed(range(dp)):
        j = onward(s)
        part_f[...] = jnp.dot(hidden, wd[:, cols(j)], preferred_element_type=F32)
        target = part_s if s > 0 else part_r

        def split(d):
            g = lax.rem(me_e + d, experts)
            start = pl.multiple_of(g * padded, 8)
            target[s, g] = part_f[pl.ds(start, slots), :].astype(BF16)
            if s > 0:
                to_dp(part_s.at[s, g], part_r.at[s, g], s4.at[s, d], r4.at[s, d], s).start()

        each_from(1, experts, split)
        split(0)

    def summed(d):
        g = lax.rem(me_e + d, experts)
        for s in range(1, dp):
            to_dp(part_s.at[s, g], part_r.at[s, g], s4.at[s, d], r4.at[s, d], s).wait_recv()
        value = part_r[0, g].astype(F32)
        for s in range(1, dp):
            value = value + part_r[s, g].astype(F32)
        return value.astype(BF16)

    def give(d):
        g = lax.rem(me_e + d, experts)
        back_s[g] = summed(d)
        to_expert(back_s.at[g], back_r.at[me_e], s5.at[d], r5.at[d], d).start()

    each_from(1, experts, give)
    back_r[me_e] = summed(0)

    def collect(d):
        e = lax.rem(me_e + experts - d, experts)
        to_expert(back_s.at[e], back_r.at[e], s5.at[d], r5.at[d], d).wait_recv()

    each_from(1, experts, collect)

    def place(e):
        rows_f[pl.ds(e * padded, slots), :] = back_r[e].astype(F32)

    each(experts, place)
    group_x[...] = lax.dot_general(wsel[...].astype(BF16), rows_f[...].astype(BF16), (((0,), (0,)), ((), ())),
                                   preferred_element_type=F32)
    for j in range(dp):
        mix_s[j] = group_x[j * own:(j + 1) * own, :].astype(BF16)
    for s in reversed(range(1, dp)):
        to_dp(mix_s.at[onward(s)], out.at[:, cols(me_j)], s6.at[s], r6.at[s], s).start()
    kept = pltpu.make_async_copy(mix_s.at[me_j], out.at[:, cols(me_j)], s6.at[0])
    kept.start()
    kept.wait()
    for s in range(1, dp):
        j = backward(s)
        to_dp(mix_s.at[j], out.at[:, cols(j)], s6.at[s], r6.at[s], s).wait_recv()

    for s in range(1, dp):
        to_dp(info_s, info_r.at[s], si.at[s], ri.at[s], s).wait_send()
        to_dp(tok_s.at[s], tok_r.at[me_j], s1.at[s], r1.at[s], s).wait_send()
        to_dp(mix_s.at[onward(s)], out.at[:, cols(me_j)], s6.at[s], r6.at[s], s).wait_send()

    def left(d):
        g = lax.rem(me_e + experts - d, experts)
        for s in range(1, dp):
            to_dp(rows_r.at[me_j, g], rows_r.at[me_j, g], s3.at[s, d], r3.at[s, d], s).wait_send()
            to_dp(part_s.at[s, g], part_r.at[s, g], s4.at[s, d], r4.at[s, d], s).wait_send()

    def left_expert(d):
        e = lax.rem(me_e + d, experts)
        to_expert(disp_s.at[e], rows_r.at[me_j, me_e], s2.at[d], r2.at[d], d).wait_send()
        to_expert(back_s.at[e], back_r.at[me_e], s5.at[d], r5.at[d], d).wait_send()

    each(experts, left)
    each_from(1, experts, left_expert)


def body(tokens, expert_ids, gate_weights, placement, w_gate, w_up, w_down):
    experts = lax.axis_size("expert")
    dp = lax.axis_size("dp")
    own, width = tokens.shape
    topk = expert_ids.shape[1]
    group = own * dp
    first = max(2, group * topk // experts)
    slots = first + max(1, first // 2)
    padded = -(-slots // 8) * 8
    lanes = -(-group * topk // 128) * 128
    block = width // dp
    units = w_gate.shape[1]
    total = experts * padded
    hbm = pl.BlockSpec(memory_space=pl.ANY)
    dma = pltpu.SemaphoreType.DMA
    return pl.pallas_call(
        functools.partial(kernel, experts, dp, topk, first, slots, padded),
        out_shape=jax.ShapeDtypeStruct((own, width), BF16),
        in_specs=[hbm] * 7,
        out_specs=hbm,
        scratch_shapes=[
            pltpu.VMEM((own, width), BF16),
            pltpu.VMEM((topk, own), jnp.int32),
            pltpu.VMEM((topk, own), BF16),
            pltpu.VMEM(placement.shape, jnp.int32),
            pltpu.VMEM((units, width), BF16),
            pltpu.VMEM((units, width), BF16),
            pltpu.VMEM((units, width), BF16),
            pltpu.VMEM((dp, own, block), BF16),
            pltpu.VMEM((dp, own, block), BF16),
            pltpu.VMEM((8, lanes), F32),
            pltpu.VMEM((dp, 8, lanes), F32),
            pltpu.VMEM((group, block), F32),
            pltpu.VMEM((experts, slots, block), BF16),
            pltpu.VMEM((dp, experts, slots, block), BF16),
            pltpu.VMEM((total, block), F32),
            pltpu.VMEM((total, block), F32),
            pltpu.VMEM((dp, experts, slots, block), BF16),
            pltpu.VMEM((dp, experts, slots, block), BF16),
            pltpu.VMEM((experts, slots, block), BF16),
            pltpu.VMEM((experts, slots, block), BF16),
            pltpu.VMEM((total, group), F32),
            pltpu.VMEM((dp, own, block), BF16),
            dma((7,)),
            dma((dp,)), dma((dp,)), dma((dp,)), dma((dp,)),
            dma((experts,)), dma((experts,)),
            dma((dp, experts)), dma((dp, experts)),
            dma((dp, experts)), dma((dp, experts)),
            dma((experts,)), dma((experts,)),
            dma((dp,)), dma((dp,)),
        ],
        compiler_params=pltpu.CompilerParams(
            collective_id=0, has_side_effects=True, vmem_limit_bytes=56 << 20
        ),
    )(tokens, expert_ids.T, gate_weights.T, placement, w_gate[0], w_up[0], w_down[0])


def solution(mesh):
    placed = (
        P(("groups", "expert", "dp"), None),
        P(("groups", "expert", "dp"), None),
        P(("groups", "expert", "dp"), None),
        P("groups", None),
        P("expert", "dp", None),
        P("expert", "dp", None),
        P("expert", "dp", None),
    )
    return jax.shard_map(
        body,
        mesh=mesh,
        in_specs=placed,
        out_specs=P(("groups", "expert", "dp"), None),
        check_vma=False,
    )
```
